768 devices in a mesh: grid: 24 (over x_hi, z), ks: 32 (over x_lo, y, core).
Axes of the slice: x: 4 (x_hi: 2, x_lo: 2; x = x_hi * 2 + x_lo), y: 8, z: 12, core: 2. Of those that a mesh axis runs over, the one named last changes fastest.
Arguments:
- orbitals: bfloat16 [32, 256, 64, 24, 128], P('ks', None, None, 'grid'), may hold values from -2 to 2
- occupied: int32 [32], replicated, may hold values from 64 to 256, as said below
- kweight: int32 [32], replicated, may hold values from 1 to 8
Outputs:
- spin_density: float32 [2, 64, 24, 128], P(None, None, 'grid')
- potential: float32 [2, 64, 24, 128], P(None, None, 'grid')
- flux: float32 [2, 64, 3, 24, 128], P(None, None, None, 'grid')
The draws below stay inside these ranges and needn't reach their ends.
Inputs may be any that keep to these rules, and one draw needn't show every extreme that they name: Some group has all 256 bands occupied.
All inputs are finite; a program needn't handle non-finite values.
Results may differ from the reference program's by a relative error of at most 0.0003.
Values sent between devices are 32-bit elements; how exact they have to be, the bound alone decides.
A program may use at most 32 MiB of HBM per device.

```python
import math
import jax
import jax.numpy as jnp
from jax import lax

BANDS = 256
NY = 64
NZ = 128
GROUPS = 32
NX = 24


def draw_orbitals(key, part):
    base_key, amp_key = jax.random.split(jax.random.fold_in(key, 11))
    shape = (GROUPS, BANDS, NY, NX, NZ)
    base = jax.random.normal(base_key, shape, jnp.float32)
    amplitude = jnp.exp(jax.random.uniform(amp_key, (2, NY, NX, NZ), jnp.float32, -1.2, 1.2))
    spin_index = jnp.arange(GROUPS) % 2
    chosen = amplitude[spin_index][:, None]
    values = jnp.clip(base * chosen * 0.0625, -2.0, 2.0)
    return values.astype(jnp.bfloat16)


def draw_occupied(key, part):
    count_key, top_key = jax.random.split(jax.random.fold_in(key, 23))
    counts = jax.random.randint(count_key, (GROUPS,), BANDS // 4, BANDS + 1)
    chosen = jax.random.randint(top_key, (), 0, GROUPS)
    return jnp.where(jnp.arange(GROUPS) == chosen, BANDS, counts).astype(jnp.int32)


def set_ends(result, rng, least, top_value):
    index_at = [jax.random.randint(jax.random.fold_in(rng, axis), (), 0, length) for axis, length in enumerate(result.shape)]
    widest = result.shape.index(max(result.shape))
    neighbour = index_at[:widest] + [(index_at[widest] + 1) % result.shape[widest]] + index_at[widest + 1:]
    return result.at[tuple(index_at)].set(least).at[tuple(neighbour)].set(top_value)


def setup_inputs(seed: int = 0) -> dict:
    key_list = jax.random.split(jax.random.key(seed), 4)
    orbitals = draw_orbitals(jax.random.fold_in(key_list[3], 71), 0)
    occupied = draw_occupied(jax.random.fold_in(key_list[3], 71), 0)
    kweight = set_ends(jax.random.randint(key_list[2], (GROUPS,), 1, 9), jax.random.fold_in(key_list[2], 1), 1, 8).astype(jnp.int32)
    return dict(orbitals=orbitals, occupied=occupied, kweight=kweight)


exchange_coef = 0.75 * (3.0 / math.pi) ** (1.0 / 3.0)
kappa_value = 0.804
mu_value = 0.2195
fermi_term = 4.0 * (3.0 * math.pi * math.pi) ** (2.0 / 3.0)

def energy_total(density, gradient):
    scaled = 2.0 * density
    square = 4.0 * lax.optimization_barrier(jnp.sum(gradient * gradient, axis=2))
    reduced = square / (fermi_term * scaled ** (8.0 / 3.0))
    enhance = 1.0 + kappa_value - kappa_value / (1.0 + mu_value * reduced / kappa_value)
    exchange = -0.5 * exchange_coef * scaled ** (4.0 / 3.0) * enhance
    total = density[0] + density[1]
    polar = (density[0] - density[1]) / total
    radius = (3.0 / (4.0 * math.pi * total)) ** (1.0 / 3.0)
    correl = -total * 0.44 / (radius + 7.8) * (1.0 - 0.5 * polar * polar)
    return jnp.sum(exchange) + jnp.sum(correl)

def reference(orbitals, occupied, kweight):
    groups = occupied.shape[0]
    weights = kweight.astype(jnp.float32)
    up_total = jnp.sum(weights[0::2])
    down_total = jnp.sum(weights[1::2])
    spin_up = jnp.arange(groups) % 2 == 0
    scale = weights / jnp.where(spin_up, up_total, down_total)
    bands = jnp.arange(orbitals.shape[1], dtype=jnp.int32)
    coef = jnp.where(bands[None, :] < occupied[:, None], scale[:, None], 0.0).astype(jnp.float32)
    upper = spin_up.astype(jnp.float32)

    def add_group(carry, items):
        orbit, factor, is_upper = items
        values = orbit.astype(jnp.float32)
        term = jnp.tensordot(factor, values * values, axes=1, precision=lax.Precision.HIGHEST)
        return (carry + jnp.stack([term * is_upper, term * (1.0 - is_upper)]), None)
    start = jnp.zeros((2,) + orbitals.shape[2:], jnp.float32)
    density, unused = lax.scan(add_group, start, (orbitals, coef, upper))
    grad_y = (jnp.roll(density, -1, 1) - jnp.roll(density, 1, 1)) * 0.5
    grad_x = (jnp.roll(density, -1, 2) - jnp.roll(density, 1, 2)) * 0.5
    grad_z = (jnp.roll(density, -1, 3) - jnp.roll(density, 1, 3)) * 0.5
    gradient = jnp.stack([grad_y, grad_x, grad_z], axis=2)
    potential, flux = jax.grad(energy_total, argnums=(0, 1))(density, gradient)
    return (density, potential, flux)
```

```python
import functools
import math

import jax
import jax.numpy as jnp
from jax import lax
from jax.experimental import pallas as pl
from jax.experimental.pallas import tpu as pltpu
from jax.sharding import PartitionSpec as P

MESH = pl.DeviceIdType.MESH
CHUNKS = 8

exchange_coef = 0.75 * (3.0 / math.pi) ** (1.0 / 3.0)
kappa_value = 0.804
mu_value = 0.2195
fermi_term = 4.0 * (3.0 * math.pi * math.pi) ** (2.0 / 3.0)
radius_coef = (3.0 / (4.0 * math.pi)) ** (1.0 / 3.0)


def gather_kernel(
    sizes, orb_hbm, occ_hbm, kw_hbm, dens_ref, grad_ref,
    orb, occ, kw, part, recv, mine, halo, slope,
    load_sem, scalar_sem, rs_send, rs_recv, swap_send, swap_recv, halo_send, halo_recv, ag_send, ag_recv,
):
    n_grid, n_chip, n_y, n_z, bands = sizes
    n_x = n_chip // n_y
    g = lax.axis_index("grid")
    k = lax.axis_index("ks")
    core = k % 2
    chip = k // 2
    cx, cy = chip // n_y, chip % n_y
    block = bands // CHUNKS

    loads = [
        pltpu.make_async_copy(orb_hbm.at[pl.ds(i * block, block)], orb.at[pl.ds(i * block, block)], load_sem.at[i])
        for i in range(CHUNKS)
    ]
    scalars = [
        pltpu.make_async_copy(occ_hbm, occ, scalar_sem.at[0]),
        pltpu.make_async_copy(kw_hbm, kw, scalar_sem.at[1]),
    ]
    for copy in scalars + loads:
        copy.start()

    def shard_of(x, y, grid):
        return (x + grid // n_z) % n_x * n_y + y

    own = shard_of(cx, cy, g)

    steps = sorted(
        ((dx, dy) for dx in range(n_x) for dy in range(n_y) if dx or dy),
        key=lambda s: (-(s[0] + min(s[1], n_y - s[1])), s),
    )
    peers = []
    for dx, dy in steps:
        x, y = (cx + dx) % n_x, (cy + dy) % n_y
        peers.append(((x * n_y + y) * 2 + core, shard_of(x, y, g)))
    sides = []
    for d in (1, n_grid - 1):
        side = (g + d) % n_grid
        x = (own // n_y + side // n_z) % n_x
        sides.append((side, (x * n_y + cy) * 2))
    partner = chip * 2 + 1 - core

    barrier = pltpu.get_barrier_semaphore()
    for peer, _ in peers:
        pl.semaphore_signal(barrier, inc=1, device_id=(g, peer), device_id_type=MESH)
    for side, base in sides:
        for c in range(2):
            pl.semaphore_signal(barrier, inc=1, device_id=(side, base + c), device_id_type=MESH)
    pl.semaphore_signal(barrier, inc=1, device_id=(g, partner), device_id_type=MESH)

    for copy in scalars:
        copy.wait()
    count = occ[k]
    whole = kw[core]
    for i in range(1, kw.shape[0] // 2):
        whole = whole + kw[2 * i + core]
    shape = part.shape
    flat = (shape[0] * shape[1], shape[2])
    scale = jnp.full(flat, kw[k], jnp.int32).astype(jnp.float32) / jnp.full(flat, whole, jnp.int32).astype(jnp.float32)

    total = jnp.zeros(flat, jnp.float32)
    for i in range(CHUNKS):
        loads[i].wait()

        def add(b, acc):
            values = orb[b].astype(jnp.float32)
            return acc + jnp.where(b < count, values * values, 0.0)

        total = lax.fori_loop(i * block, (i + 1) * block, add, total, unroll=8)
    total = total * scale
    for j in range(shape[0]):
        part[j] = total[j * shape[1]:(j + 1) * shape[1]]

    pl.semaphore_wait(barrier, len(peers) + 5)

    def send(src, dst, send_sem, recv_sem, device):
        copy = pltpu.make_async_remote_copy(
            src_ref=src, dst_ref=dst, send_sem=send_sem, recv_sem=recv_sem, device_id=device, device_id_type=MESH
        )
        copy.start()
        return copy

    def wait_for(ref, sem):
        pltpu.make_async_copy(ref, ref, sem).wait()

    for i, (peer, shard) in enumerate(peers):
        send(part.at[shard], recv.at[i], rs_send, rs_recv, (g, peer))
    result = part[own]
    wait_for(recv, rs_recv)
    for i in range(len(peers)):
        result = result + recv[i]
    mine[core] = result

    for d, (side, base) in enumerate(sides):
        for c in range(2):
            send(mine.at[core], halo.at[1 - d, core], halo_send, halo_recv, (side, base + c))
    swap = send(mine.at[core], mine.at[core], swap_send, swap_recv, (g, partner))
    swap.wait()
    for peer, _ in peers:
        send(mine, dens_ref.at[:, own], ag_send.at[0], ag_recv.at[0], (g, peer))
    dens_ref[:, own] = mine[...]
    wait_for(halo, halo_recv)
    slope[...] = (halo[0] - halo[1]) * 0.5
    for peer, _ in peers:
        send(slope, grad_ref.at[:, own], ag_send.at[1], ag_recv.at[1], (g, peer))
    grad_ref[:, own] = slope[...]

    wait_for(recv, rs_send)
    wait_for(halo, halo_send)
    rest = pl.ds(0, len(peers))
    for i, ref in enumerate((dens_ref, grad_ref)):
        wait_for(ref.at[:, rest], ag_send.at[i])
        wait_for(ref.at[:, rest], ag_recv.at[i])


def energy_kernel(dens_ref, grad_ref, dens_out, pot_out, flux_out):
    rows, depth = dens_ref.shape[1:]
    up, down = dens_ref[0], dens_ref[1]
    dens_out[pl.ds(0, rows)] = up
    dens_out[pl.ds(rows, rows)] = down
    both = up + down
    polar = (up - down) / both
    radius = radius_coef * jnp.exp(jnp.log(both) * (-1.0 / 3.0))
    inverse = 1.0 / (radius + 7.8)
    front = -0.44 * inverse
    even = (1.0 - 0.5 * polar * polar) * (1.0 + radius * inverse * (1.0 / 3.0))
    for s, (value, sign) in enumerate(((up, 1.0), (down, -1.0))):
        scaled = 2.0 * value
        cube = jnp.exp(jnp.log(scaled) * (1.0 / 3.0))
        power = scaled * cube
        over = 1.0 / power
        grad_y = (pltpu.roll(value, rows - 1, 0) - pltpu.roll(value, 1, 0)) * 0.5
        grad_z = (pltpu.roll(value, depth - 1, 1) - pltpu.roll(value, 1, 1)) * 0.5
        grad_x = grad_ref[s]
        square = 4.0 * (grad_y * grad_y + grad_x * grad_x + grad_z * grad_z)
        reduced = square * over * over * (1.0 / fermi_term)
        ratio = 1.0 / (1.0 + (mu_value / kappa_value) * reduced)
        enhance = 1.0 + kappa_value - kappa_value * ratio
        slope = mu_value * ratio
        exchange = -exchange_coef * cube * (
            (4.0 / 3.0) * enhance - (8.0 / 3.0) * (reduced * ratio) * slope
        )
        pot_out[pl.ds(s * rows, rows)] = exchange + front * (even - polar * (sign - polar))
        factor = (-4.0 * exchange_coef / fermi_term) * (slope * ratio) * over
        for c, part in enumerate((grad_y, grad_x, grad_z)):
            flux_out[pl.ds(s * 3 * rows + c, rows, stride=3)] = factor * part


def on_device(n_grid, n_chip, n_y, n_z, orbitals, occupied, kweight):
    _, bands, rows, _, depth = orbitals.shape
    local = orbitals.reshape(bands, rows, depth)
    shard = rows // n_chip
    out = jax.ShapeDtypeStruct((2, n_chip, shard, depth), jnp.float32)
    vmem = pl.BlockSpec(memory_space=pltpu.VMEM)
    dma = pltpu.SemaphoreType.DMA
    dens, grad = pl.pallas_call(
        functools.partial(gather_kernel, (n_grid, n_chip, n_y, n_z, bands)),
        out_shape=(out, out),
        in_specs=[pl.BlockSpec(memory_space=pl.ANY)] * 3,
        out_specs=(vmem, vmem),
        scratch_shapes=[
            pltpu.VMEM((bands, rows, depth), jnp.bfloat16),
            pltpu.SMEM(occupied.shape, jnp.int32),
            pltpu.SMEM(kweight.shape, jnp.int32),
            pltpu.VMEM((n_chip, shard, depth), jnp.float32),
            pltpu.VMEM((n_chip - 1, shard, depth), jnp.float32),
            pltpu.VMEM((2, shard, depth), jnp.float32),
            pltpu.VMEM((2, 2, shard, depth), jnp.float32),
            pltpu.VMEM((2, shard, depth), jnp.float32),
            dma((CHUNKS,)),
            dma((2,)),
            dma(()),
            dma(()),
            dma(()),
            dma(()),
            dma(()),
            dma(()),
            dma((2,)),
            dma((2,)),
        ],
        compiler_params=pltpu.CompilerParams(collective_id=0, has_side_effects=True),
        name="density",
    )(local, occupied, kweight)
    dens, grad = dens.reshape(2, rows, depth), grad.reshape(2, rows, depth)
    flat = functools.partial(jax.ShapeDtypeStruct, dtype=jnp.float32)
    outs = pl.pallas_call(
        energy_kernel,
        out_shape=(flat((2 * rows, depth)), flat((2 * rows, depth)), flat((6 * rows, depth))),
        in_specs=[vmem, vmem],
        out_specs=(vmem, vmem, vmem),
        name="energy",
    )(dens, grad)
    return (
        outs[0].reshape(2, rows, 1, depth),
        outs[1].reshape(2, rows, 1, depth),
        outs[2].reshape(2, rows, 3, 1, depth),
    )


def solution(mesh):
    n_grid, n_ks = mesh.shape["grid"], mesh.shape["ks"]
    placed = (P("ks", None, None, "grid", None), P(), P())
    return jax.shard_map(
        functools.partial(on_device, n_grid, n_ks // 2, 8, 12),
        mesh=mesh,
        in_specs=placed,
        out_specs=(
            P(None, None, "grid", None),
            P(None, None, "grid", None),
            P(None, None, None, "grid", None),
        ),
        check_vma=False,
    )
```

```python
import functools
import math

import jax
import jax.numpy as jnp
from jax import lax
from jax.experimental import pallas as pl
from jax.experimental.pallas import tpu as pltpu
from jax.sharding import PartitionSpec as P

MESH = pl.DeviceIdType.MESH
CHUNKS = 4
UNROLL = 8
VMEM_LIMIT = 62 << 20

exchange_coef = 0.75 * (3.0 / math.pi) ** (1.0 / 3.0)
kappa_value = 0.804
mu_value = 0.2195
fermi_term = 4.0 * (3.0 * math.pi * math.pi) ** (2.0 / 3.0)
radius_coef = (3.0 / (4.0 * math.pi)) ** (1.0 / 3.0)


def gather_kernel(
    sizes, orb_hbm, occ_hbm, kw_hbm, dens_ref, grad_ref,
    orb, occ, kw, part, recv, mine,
    load_sem, scalar_sem, rs_send, rs_recv, reply_send, reply_recv, ag_send, ag_recv, known,
):
    n_grid, n_x, n_y, n_z = sizes
    bands, rows = orb_hbm.shape[:2]
    g = lax.axis_index("grid")
    k = lax.axis_index("ks")
    core = k % 2
    chip = k // 2
    cx, cy = chip // n_y, chip % n_y
    z = g % n_z
    first, last = z == 0, z == n_z - 1
    after, before = (g + 1) % n_grid, (g + n_grid - 1) % n_grid
    tile = rows // n_y
    thick = rows // CHUNKS
    tiles = n_y // CHUNKS
    FROM_AFTER, FROM_OWN, FROM_BEFORE = 0, 1, 2
    OWN, NEXT, PREVIOUS, SLOPE = 0, 1, 2, 3

    turns = sorted(range(CHUNKS), key=lambda m: -min(m, CHUNKS - m))
    chunks = [(cy // tiles + m) % CHUNKS for m in turns]
    loads = [
        pltpu.make_async_copy(
            orb_hbm.at[:, pl.ds(pl.multiple_of(m * thick, thick), thick)], orb.at[i], load_sem.at[i]
        )
        for i, m in enumerate(chunks)
    ]
    scalars = [
        pltpu.make_async_copy(occ_hbm, occ, scalar_sem.at[0]),
        pltpu.make_async_copy(kw_hbm, kw, scalar_sem.at[1]),
    ]
    for copy in loads[:1] + scalars + loads[1:]:
        copy.start()

    def index(x, y, c):
        return ((x % n_x) * n_y + y % n_y) * 2 + c

    partner = index(cx, cy, 1 - core)
    column = [
        (dy, c) for dy in sorted(range(n_y), key=lambda d: -min(d, n_y - d)) for c in range(2) if dy or c
    ]
    barrier = pltpu.get_barrier_semaphore()

    def greet(grid, peer):
        pl.semaphore_signal(barrier, inc=1, device_id=(grid, peer), device_id_type=MESH)

    @pl.when(first)
    def _():
        for dx in range(n_x):
            for dy in range(n_y):
                greet(before, index(cx + dx, cy + dy, core))
        for dy, c in column:
            greet(g, index(cx, cy + dy, (core + c) % 2))
        for dy in range(n_y):
            greet(g, index(cx + 1, cy + dy, core))

    @pl.when(z > 0)
    def _():
        greet(g, partner)

    @pl.when(z < n_z - 1)
    def _():
        for dx in range(n_x):
            for dy in range(n_y):
                greet(after, index(cx + dx, cy + dy, core))

    for copy in scalars:
        copy.wait()
    count = occ[k]
    whole = kw[core]
    for i in range(1, kw.shape[0] // 2):
        whole = whole + kw[2 * i + core]
    shape = (thick, mine.shape[2])
    scale = jnp.full(shape, kw[k], jnp.int32).astype(jnp.float32) / jnp.full(shape, whole, jnp.int32).astype(jnp.float32)

    def send(src, dst, send_sem, recv_sem, device):
        copy = pltpu.make_async_remote_copy(
            src_ref=src, dst_ref=dst, send_sem=send_sem, recv_sem=recv_sem, device_id=device, device_id_type=MESH
        )
        copy.start()

    def wait_for(ref, sem):
        pltpu.make_async_copy(ref, ref, sem).wait()

    target = jnp.where(first, g, before)
    source = jnp.where(first, FROM_OWN, FROM_AFTER)
    lanes = 4
    for i, m in enumerate(chunks):
        loads[i].wait()

        def add(step, sums):
            out = list(sums)
            for j in range(UNROLL):
                b = step * UNROLL + j
                values = orb[i, b].astype(jnp.float32)
                out[j % lanes] = out[j % lanes] + jnp.where(b < count, values * values, 0.0)
            return tuple(out)

        sums = lax.fori_loop(0, bands // UNROLL, add, (jnp.zeros(shape, jnp.float32),) * lanes)
        total = ((sums[0] + sums[1]) + (sums[2] + sums[3])) * scale
        for j in range(tiles):
            part[m * tiles + j] = total[j * tile:(j + 1) * tile]
        if i == 0:
            pl.semaphore_wait(
                barrier, jnp.where(first, 3 * n_y - 1, jnp.where(last, 2 * n_x * n_y + 1, n_x * n_y + 1))
            )

        @pl.when(last)
        def _():
            for j in range(tiles):
                to = m * tiles + j
                slot = (to - cy + n_y) % n_y
                for dx in range(n_x):
                    send(
                        part.at[to], recv.at[FROM_BEFORE, dx * n_y + slot], rs_send, rs_recv.at[FROM_BEFORE],
                        (after, index(cx + dx, to, core)),
                    )

        for j in range(tiles):
            to = m * tiles + j
            slot = (to - cy + n_y) % n_y
            send(
                part.at[to], recv.at[source, n_y + slot], rs_send, rs_recv.at[source],
                (target, index(cx + 1, to, core)),
            )

            @pl.when((z > 0) | (to != cy))
            def _():
                send(
                    part.at[to], recv.at[source, slot], rs_send, rs_recv.at[source],
                    (target, index(cx, to, core)),
                )

    whole_set = pl.ds(0, n_x * n_y)
    others = pl.ds(1, n_x * n_y - 1)

    def add_up(which, value):
        for i in range(1, n_x * n_y):
            value = value + recv[which, i]
        return value

    def reply(which, src, dst, grid, x):
        send(
            mine.at[src], mine.at[dst], reply_send.at[which], reply_recv.at[which], (grid, index(x, cy, core))
        )

    def spread(i, src, ref):
        for dy, c in column:
            send(mine.at[src], ref.at[core, cy], ag_send.at[i], ag_recv.at[i], (g, index(cx, cy + dy, (core + c) % 2)))
        ref[core, cy] = mine[src]

    @pl.when(z < n_z - 1)
    def _():
        wait_for(recv.at[FROM_AFTER, whole_set], rs_recv.at[FROM_AFTER])
        mine[NEXT] = add_up(FROM_AFTER, recv[FROM_AFTER, 0])
        reply(0, NEXT, OWN, after, cx)

    @pl.when(first)
    def _():
        wait_for(recv.at[FROM_OWN, others], rs_recv.at[FROM_OWN])
        mine[OWN] = add_up(FROM_OWN, part[cy])

    @pl.when(z > 0)
    def _():
        wait_for(mine.at[OWN], reply_recv.at[0])

    pl.semaphore_signal(known, inc=1, device_id=(g, partner), device_id_type=MESH)

    @pl.when(z < n_z - 1)
    def _():
        reply(1, OWN, PREVIOUS, after, cx)

    pl.semaphore_wait(known, 1)
    spread(0, OWN, dens_ref)

    @pl.when(last)
    def _():
        wait_for(mine.at[NEXT], reply_recv.at[2])

    @pl.when(first)
    def _():
        wait_for(recv.at[FROM_BEFORE, whole_set], rs_recv.at[FROM_BEFORE])
        mine[PREVIOUS] = add_up(FROM_BEFORE, recv[FROM_BEFORE, 0])

    @pl.when(z > 0)
    def _():
        wait_for(mine.at[PREVIOUS], reply_recv.at[1])

    mine[SLOPE] = (mine[NEXT] - mine[PREVIOUS]) * 0.5
    spread(1, SLOPE, grad_ref)

    @pl.when(first)
    def _():
        reply(2, OWN, NEXT, before, cx + 1)
        wait_for(mine.at[OWN], reply_send.at[2])
        wait_for(recv.at[FROM_OWN, others], rs_send)

    @pl.when(z < n_z - 1)
    def _():
        wait_for(mine.at[OWN], reply_send.at[0])
        wait_for(mine.at[OWN], reply_send.at[1])

    @pl.when(z > 0)
    def _():
        wait_for(recv.at[FROM_OWN, whole_set], rs_send)

    @pl.when(last)
    def _():
        wait_for(recv.at[FROM_OWN, whole_set], rs_send)

    for i in range(2):
        wait_for(recv.at[FROM_OWN, others], ag_send.at[i])
        wait_for(recv.at[FROM_OWN, others], ag_recv.at[i])


def energy_kernel(dens_ref, grad_ref, dens_out, pot_out, flux_out):
    rows, depth = dens_ref.shape[1:]
    up, down = dens_ref[0], dens_ref[1]
    dens_out[pl.ds(0, rows)] = up
    dens_out[pl.ds(rows, rows)] = down
    both = up + down
    polar = (up - down) / both
    radius = radius_coef * jnp.exp(jnp.log(both) * (-1.0 / 3.0))
    inverse = 1.0 / (radius + 7.8)
    front = -0.44 * inverse
    even = (1.0 - 0.5 * polar * polar) * (1.0 + radius * inverse * (1.0 / 3.0))
    for s, (value, sign) in enumerate(((up, 1.0), (down, -1.0))):
        scaled = 2.0 * value
        cube = jnp.exp(jnp.log(scaled) * (1.0 / 3.0))
        power = scaled * cube
        over = 1.0 / power
        grad_y = (pltpu.roll(value, rows - 1, 0) - pltpu.roll(value, 1, 0)) * 0.5
        grad_z = (pltpu.roll(value, depth - 1, 1) - pltpu.roll(value, 1, 1)) * 0.5
        grad_x = grad_ref[s]
        square = 4.0 * (grad_y * grad_y + grad_x * grad_x + grad_z * grad_z)
        reduced = square * over * over * (1.0 / fermi_term)
        ratio = 1.0 / (1.0 + (mu_value / kappa_value) * reduced)
        enhance = 1.0 + kappa_value - kappa_value * ratio
        slope = mu_value * ratio
        exchange = -exchange_coef * cube * (
            (4.0 / 3.0) * enhance - (8.0 / 3.0) * (reduced * ratio) * slope
        )
        pot_out[pl.ds(s * rows, rows)] = exchange + front * (even - polar * (sign - polar))
        factor = (-4.0 * exchange_coef / fermi_term) * (slope * ratio) * over
        for c, part in enumerate((grad_y, grad_x, grad_z)):
            flux_out[pl.ds(s * 3 * rows + c, rows, stride=3)] = factor * part


def on_device(n_grid, n_x, n_y, n_z, orbitals, occupied, kweight):
    _, bands, rows, _, depth = orbitals.shape
    local = orbitals.reshape(bands, rows, depth)
    tile = rows // n_y
    out = pltpu.VMEM((2, n_y, tile, depth), jnp.float32)
    vmem = pl.BlockSpec(memory_space=pltpu.VMEM)
    dma = pltpu.SemaphoreType.DMA
    dens, grad = pl.pallas_call(
        functools.partial(gather_kernel, (n_grid, n_x, n_y, n_z)),
        out_shape=(out, out),
        in_specs=[pl.BlockSpec(memory_space=pl.ANY)] * 3,
        out_specs=(vmem, vmem),
        scratch_shapes=[
            pltpu.VMEM((CHUNKS, bands, rows // CHUNKS, depth), jnp.bfloat16),
            pltpu.SMEM(occupied.shape, jnp.int32),
            pltpu.SMEM(kweight.shape, jnp.int32),
            pltpu.VMEM((n_y, tile, depth), jnp.float32),
            pltpu.VMEM((3, 2 * n_y, tile, depth), jnp.float32),
            pltpu.VMEM((4, tile, depth), jnp.float32),
            dma((CHUNKS,)),
            dma((2,)),
            dma(()),
            dma((3,)),
            dma((3,)),
            dma((3,)),
            dma((2,)),
            dma((2,)),
            pltpu.SemaphoreType.REGULAR,
        ],
        compiler_params=pltpu.CompilerParams(
            collective_id=0, has_side_effects=True, vmem_limit_bytes=VMEM_LIMIT
        ),
        name="density",
    )(local, occupied, kweight)
    dens, grad = dens.reshape(2, rows, depth), grad.reshape(2, rows, depth)
    flat = functools.partial(jax.ShapeDtypeStruct, dtype=jnp.float32)
    outs = pl.pallas_call(
        energy_kernel,
        out_shape=(flat((2 * rows, depth)), flat((2 * rows, depth)), flat((6 * rows, depth))),
        in_specs=[vmem, vmem],
        out_specs=(vmem, vmem, vmem),
        compiler_params=pltpu.CompilerParams(vmem_limit_bytes=8 << 20),
        name="energy",
    )(dens, grad)
    return (
        outs[0].reshape(2, rows, 1, depth),
        outs[1].reshape(2, rows, 1, depth),
        outs[2].reshape(2, rows, 3, 1, depth),
    )


def solution(mesh):
    n_grid, n_ks = mesh.shape["grid"], mesh.shape["ks"]
    placed = (P("ks", None, None, "grid", None), P(), P())
    return jax.shard_map(
        functools.partial(on_device, n_grid, 2, n_ks // 4, n_grid // 2),
        mesh=mesh,
        in_specs=placed,
        out_specs=(
            P(None, None, "grid", None),
            P(None, None, "grid", None),
            P(None, None, None, "grid", None),
        ),
        check_vma=False,
    )
```

```python
import functools
import math

import jax
import jax.numpy as jnp
from jax import lax
from jax.experimental import pallas as pl
from jax.experimental.pallas import tpu as pltpu
from jax.sharding import PartitionSpec as P

MESH = pl.DeviceIdType.MESH
CHUNKS = 4
UNROLL = 8
VMEM_LIMIT = 62 << 20

exchange_coef = 0.75 * (3.0 / math.pi) ** (1.0 / 3.0)
kappa_value = 0.804
mu_value = 0.2195
fermi_term = 4.0 * (3.0 * math.pi * math.pi) ** (2.0 / 3.0)
radius_coef = (3.0 / (4.0 * math.pi)) ** (1.0 / 3.0)


def gather_kernel(
    sizes, orb_hbm, occ_hbm, kw_hbm, dens_ref, grad_ref,
    *scratch,
):
    orb = scratch[:CHUNKS]
    (
        occ, kw, part, recv, mine,
        load_sem, scalar_sem, rs_send, rs_recv, reply_send, reply_recv, ag_send, ag_recv, known,
    ) = scratch[CHUNKS:]
    n_grid, n_x, n_y, n_z = sizes
    bands, rows = orb_hbm.shape[:2]
    g = lax.axis_index("grid")
    k = lax.axis_index("ks")
    core = k % 2
    chip = k // 2
    cx, cy = chip // n_y, chip % n_y
    z = g % n_z
    first, last = z == 0, z == n_z - 1
    after, before = (g + 1) % n_grid, (g + n_grid - 1) % n_grid
    tile = rows // n_y
    thick = rows // CHUNKS
    tiles = n_y // CHUNKS
    FROM_AFTER, FROM_OWN, FROM_BEFORE = 0, 1, 2
    OWN, NEXT, PREVIOUS, SLOPE = 0, 1, 2, 3

    turns = sorted(range(CHUNKS), key=lambda m: -min(m, CHUNKS - m))
    chunks = [(cy // tiles + m) % CHUNKS for m in turns]
    loads = [
        pltpu.make_async_copy(
            orb_hbm.at[:, pl.ds(pl.multiple_of(m * thick, thick), thick)], orb[i], load_sem.at[i]
        )
        for i, m in enumerate(chunks)
    ]
    scalars = [
        pltpu.make_async_copy(occ_hbm, occ, scalar_sem.at[0]),
        pltpu.make_async_copy(kw_hbm, kw, scalar_sem.at[1]),
    ]
    for copy in loads[:1] + scalars + loads[1:]:
        copy.start()

    def index(x, y, c):
        return ((x % n_x) * n_y + y % n_y) * 2 + c

    partner = index(cx, cy, 1 - core)
    column = [
        (dy, c) for dy in sorted(range(n_y), key=lambda d: -min(d, n_y - d)) for c in range(2) if dy or c
    ]
    barrier = pltpu.get_barrier_semaphore()

    def greet(grid, peer):
        pl.semaphore_signal(barrier, inc=1, device_id=(grid, peer), device_id_type=MESH)

    @pl.when(first)
    def _():
        for dx in range(n_x):
            for dy in range(n_y):
                greet(before, index(cx + dx, cy + dy, core))
        for dy, c in column:
            greet(g, index(cx, cy + dy, (core + c) % 2))
        for dy in range(n_y):
            greet(g, index(cx + 1, cy + dy, core))

    @pl.when(z > 0)
    def _():
        greet(g, partner)

    @pl.when(z < n_z - 2)
    def _():
        for dx in range(n_x):
            for dy in range(n_y):
                greet(after, index(cx + dx, cy + dy, core))

    @pl.when(z == n_z - 2)
    def _():
        greet(after, k)

    for copy in scalars:
        copy.wait()
    count = occ[k]
    whole = kw[core]
    for i in range(1, kw.shape[0] // 2):
        whole = whole + kw[2 * i + core]
    shape = (thick, mine.shape[2])
    scale = jnp.full(shape, kw[k], jnp.int32).astype(jnp.float32) / jnp.full(shape, whole, jnp.int32).astype(jnp.float32)

    def send(src, dst, send_sem, recv_sem, device):
        copy = pltpu.make_async_remote_copy(
            src_ref=src, dst_ref=dst, send_sem=send_sem, recv_sem=recv_sem, device_id=device, device_id_type=MESH
        )
        copy.start()

    def wait_for(ref, sem):
        pltpu.make_async_copy(ref, ref, sem).wait()

    target = jnp.where(first, g, jnp.where(last, after, before))
    source = jnp.where(first, FROM_OWN, jnp.where(last, FROM_BEFORE, FROM_AFTER))
    groups = count // UNROLL
    rest = jnp.minimum(groups * UNROLL, bands - UNROLL)

    def pair_sum(values):
        while len(values) > 1:
            values = [a + b for a, b in zip(values[::2], values[1::2])]
        return values[0]

    for i, m in enumerate(chunks):
        loads[i].wait()

        def add(step, sums):
            values = [orb[i][step * UNROLL + j].astype(jnp.float32) for j in range(UNROLL)]
            group = pair_sum([v * v for v in values])
            return sums + jnp.where(step < groups, group, 0.0)

        total = lax.fori_loop(0, bands // UNROLL, add, jnp.zeros(shape, jnp.float32), unroll=2)
        values = [orb[i][rest + j].astype(jnp.float32) for j in range(UNROLL)]
        total = total + pair_sum([jnp.where(groups * UNROLL + j < count, v * v, 0.0) for j, v in enumerate(values)])
        total = total * scale
        for j in range(tiles):
            part[m * tiles + j] = total[j * tile:(j + 1) * tile]
        if i == 0:
            pl.semaphore_wait(
                barrier, jnp.where(first, 3 * n_y - 1, jnp.where(last, n_x * n_y + 2, n_x * n_y + 1))
            )

        for j in range(tiles):
            to = m * tiles + j
            slot = (to - cy + n_y) % n_y
            send(
                part.at[to], recv.at[source, n_y + slot], rs_send, rs_recv.at[source],
                (target, index(cx + 1, to, core)),
            )

            @pl.when((z > 0) | (to != cy))
            def _():
                send(
                    part.at[to], recv.at[source, slot], rs_send, rs_recv.at[source],
                    (target, index(cx, to, core)),
                )

    whole_set = pl.ds(0, n_x * n_y)
    others = pl.ds(1, n_x * n_y - 1)

    def add_up(which, value):
        for i in range(1, n_x * n_y):
            value = value + recv[which, i]
        return value

    def reply(which, what, src, dst, grid, x):
        send(
            mine.at[src], mine.at[dst], reply_send.at[which], reply_recv.at[what], (grid, index(x, cy, core))
        )

    def spread(i, src, ref):
        for dy, c in column:
            send(mine.at[src], ref.at[core, cy], ag_send.at[i], ag_recv.at[i], (g, index(cx, cy + dy, (core + c) % 2)))
        ref[core, cy] = mine[src]

    @pl.when(z < n_z - 2)
    def _():
        wait_for(recv.at[FROM_AFTER, whole_set], rs_recv.at[FROM_AFTER])
        mine[NEXT] = add_up(FROM_AFTER, recv[FROM_AFTER, 0])
        reply(0, 0, NEXT, OWN, after, cx)

    @pl.when(first)
    def _():
        wait_for(recv.at[FROM_OWN, others], rs_recv.at[FROM_OWN])
        mine[OWN] = add_up(FROM_OWN, part[cy])

    @pl.when(z > 0)
    def _():
        wait_for(mine.at[OWN], reply_recv.at[0])

    pl.semaphore_signal(known, inc=1, device_id=(g, partner), device_id_type=MESH)

    @pl.when(z < n_z - 2)
    def _():
        reply(1, 1, OWN, PREVIOUS, after, cx)

    @pl.when(last)
    def _():
        reply(2, 2, OWN, NEXT, before, cx)

    pl.semaphore_wait(known, 1)
    spread(0, OWN, dens_ref)

    @pl.when(z >= n_z - 2)
    def _():
        wait_for(mine.at[NEXT], reply_recv.at[2])

    @pl.when(z == n_z - 2)
    def _():
        reply(1, 1, OWN, PREVIOUS, after, cx)

    @pl.when(first)
    def _():
        wait_for(recv.at[FROM_BEFORE, whole_set], rs_recv.at[FROM_BEFORE])
        mine[PREVIOUS] = add_up(FROM_BEFORE, recv[FROM_BEFORE, 0])

    @pl.when(z > 0)
    def _():
        wait_for(mine.at[PREVIOUS], reply_recv.at[1])

    mine[SLOPE] = (mine[NEXT] - mine[PREVIOUS]) * 0.5
    spread(1, SLOPE, grad_ref)

    @pl.when(first)
    def _():
        reply(3, 0, PREVIOUS, OWN, before, cx + 1)
        reply(2, 2, OWN, NEXT, before, cx + 1)
        wait_for(mine.at[OWN], reply_send.at[3])
        wait_for(recv.at[FROM_OWN, others], rs_send)

    @pl.when(first | last)
    def _():
        wait_for(mine.at[OWN], reply_send.at[2])

    @pl.when(z < n_z - 2)
    def _():
        wait_for(mine.at[OWN], reply_send.at[0])

    @pl.when(z < n_z - 1)
    def _():
        wait_for(mine.at[OWN], reply_send.at[1])

    @pl.when(z > 0)
    def _():
        wait_for(recv.at[FROM_OWN, whole_set], rs_send)

    for i in range(2):
        wait_for(recv.at[FROM_OWN, others], ag_send.at[i])
        wait_for(recv.at[FROM_OWN, others], ag_recv.at[i])


def energy_kernel(dens_ref, grad_ref, dens_out, pot_out, flux_out):
    rows, depth = dens_ref.shape[1:]
    up, down = dens_ref[0], dens_ref[1]
    dens_out[pl.ds(0, rows)] = up
    dens_out[pl.ds(rows, rows)] = down
    both = up + down
    polar = (up - down) / both
    radius = radius_coef * jnp.exp(jnp.log(both) * (-1.0 / 3.0))
    inverse = 1.0 / (radius + 7.8)
    front = -0.44 * inverse
    even = (1.0 - 0.5 * polar * polar) * (1.0 + radius * inverse * (1.0 / 3.0))
    for s, (value, sign) in enumerate(((up, 1.0), (down, -1.0))):
        scaled = 2.0 * value
        cube = jnp.exp(jnp.log(scaled) * (1.0 / 3.0))
        power = scaled * cube
        over = 1.0 / power
        grad_y = (pltpu.roll(value, rows - 1, 0) - pltpu.roll(value, 1, 0)) * 0.5
        grad_z = (pltpu.roll(value, depth - 1, 1) - pltpu.roll(value, 1, 1)) * 0.5
        grad_x = grad_ref[s]
        square = 4.0 * (grad_y * grad_y + grad_x * grad_x + grad_z * grad_z)
        reduced = square * over * over * (1.0 / fermi_term)
        ratio = 1.0 / (1.0 + (mu_value / kappa_value) * reduced)
        enhance = 1.0 + kappa_value - kappa_value * ratio
        slope = mu_value * ratio
        exchange = -exchange_coef * cube * (
            (4.0 / 3.0) * enhance - (8.0 / 3.0) * (reduced * ratio) * slope
        )
        pot_out[pl.ds(s * rows, rows)] = exchange + front * (even - polar * (sign - polar))
        factor = (-4.0 * exchange_coef / fermi_term) * (slope * ratio) * over
        for c, part in enumerate((grad_y, grad_x, grad_z)):
            flux_out[pl.ds(s * 3 * rows + c, rows, stride=3)] = factor * part


def on_device(n_grid, n_x, n_y, n_z, orbitals, occupied, kweight):
    _, bands, rows, _, depth = orbitals.shape
    local = orbitals.reshape(bands, rows, depth)
    tile = rows // n_y
    out = pltpu.VMEM((2, n_y, tile, depth), jnp.float32)
    vmem = pl.BlockSpec(memory_space=pltpu.VMEM)
    dma = pltpu.SemaphoreType.DMA
    dens, grad = pl.pallas_call(
        functools.partial(gather_kernel, (n_grid, n_x, n_y, n_z)),
        out_shape=(out, out),
        in_specs=[pl.BlockSpec(memory_space=pl.ANY)] * 3,
        out_specs=(vmem, vmem),
        scratch_shapes=[
            *[pltpu.VMEM((bands, rows // CHUNKS, depth), jnp.bfloat16) for _ in range(CHUNKS)],
            pltpu.SMEM(occupied.shape, jnp.int32),
            pltpu.SMEM(kweight.shape, jnp.int32),
            pltpu.VMEM((n_y, tile, depth), jnp.float32),
            pltpu.VMEM((3, 2 * n_y, tile, depth), jnp.float32),
            pltpu.VMEM((4, tile, depth), jnp.float32),
            dma((CHUNKS,)),
            dma((2,)),
            dma(()),
            dma((3,)),
            dma((4,)),
            dma((3,)),
            dma((2,)),
            dma((2,)),
            pltpu.SemaphoreType.REGULAR,
        ],
        compiler_params=pltpu.CompilerParams(
            collective_id=0, has_side_effects=True, vmem_limit_bytes=VMEM_LIMIT
        ),
        name="density",
    )(local, occupied, kweight)
    dens, grad = dens.reshape(2, rows, depth), grad.reshape(2, rows, depth)
    flat = functools.partial(jax.ShapeDtypeStruct, dtype=jnp.float32)
    outs = pl.pallas_call(
        energy_kernel,
        out_shape=(flat((2 * rows, depth)), flat((2 * rows, depth)), flat((6 * rows, depth))),
        in_specs=[vmem, vmem],
        out_specs=(vmem, vmem, vmem),
        compiler_params=pltpu.CompilerParams(vmem_limit_bytes=8 << 20),
        name="energy",
    )(dens, grad)
    return (
        outs[0].reshape(2, rows, 1, depth),
        outs[1].reshape(2, rows, 1, depth),
        outs[2].reshape(2, rows, 3, 1, depth),
    )


def solution(mesh):
    n_grid, n_ks = mesh.shape["grid"], mesh.shape["ks"]
    placed = (P("ks", None, None, "grid", None), P(), P())
    return jax.shard_map(
        functools.partial(on_device, n_grid, 2, n_ks // 4, n_grid // 2),
        mesh=mesh,
        in_specs=placed,
        out_specs=(
            P(None, None, "grid", None),
            P(None, None, "grid", None),
            P(None, None, None, "grid", None),
        ),
        check_vma=False,
    )
```

```python
import functools
import math

import jax
import jax.numpy as jnp
from jax import lax
from jax.experimental import pallas as pl
from jax.experimental.pallas import tpu as pltpu
from jax.sharding import PartitionSpec as P

MESH = pl.DeviceIdType.MESH
CHUNKS = 4
UNROLL = 8
PARTS = 2
VMEM_LIMIT = 62 << 20

exchange_coef = 0.75 * (3.0 / math.pi) ** (1.0 / 3.0)
kappa_value = 0.804
mu_value = 0.2195
fermi_term = 4.0 * (3.0 * math.pi * math.pi) ** (2.0 / 3.0)
radius_coef = (3.0 / (4.0 * math.pi)) ** (1.0 / 3.0)


def gather_kernel(
    sizes, orb_hbm, occ_hbm, kw_hbm, dens_ref, pot_ref, flux_ref,
    *scratch,
):
    orb = scratch[:CHUNKS]
    (
        occ, kw, part, recv, mine, grad_ref, ready,
        load_sem, scalar_sem, rs_send, rs_recv, reply_send, reply_recv, ag_send, ag_recv, known,
    ) = scratch[CHUNKS:]
    n_grid, n_x, n_y, n_z = sizes
    bands, rows = orb_hbm.shape[:2]
    g = lax.axis_index("grid")
    k = lax.axis_index("ks")
    core = k % 2
    chip = k // 2
    cx, cy = chip // n_y, chip % n_y
    z = g % n_z
    first, last = z == 0, z == n_z - 1
    after, before = (g + 1) % n_grid, (g + n_grid - 1) % n_grid
    tile = rows // n_y
    thick = rows // CHUNKS
    tiles = n_y // CHUNKS
    FROM_AFTER, FROM_OWN, FROM_BEFORE = 0, 1, 2
    OWN, NEXT, PREVIOUS, SLOPE = 0, 1, 2, 3

    turns = sorted(range(CHUNKS), key=lambda m: -min(m, CHUNKS - m))
    chunks = [(cy // tiles + m) % CHUNKS for m in turns]
    half = bands // PARTS
    loads = [
        pltpu.make_async_copy(
            orb_hbm.at[pl.ds(p * half, half), pl.ds(pl.multiple_of(m * thick, thick), thick)],
            orb[i].at[pl.ds(p * half, half)],
            load_sem.at[i * PARTS + p],
        )
        for i, m in enumerate(chunks)
        for p in range(PARTS)
    ]
    scalars = [
        pltpu.make_async_copy(occ_hbm, occ, scalar_sem.at[0]),
        pltpu.make_async_copy(kw_hbm, kw, scalar_sem.at[1]),
    ]
    for copy in loads[:1] + scalars + loads[1:]:
        copy.start()

    def index(x, y, c):
        return (lax.rem(x, n_x) * n_y + lax.rem(y, n_y)) * 2 + c

    partner = index(cx, cy, 1 - core)
    column = [
        (dy, c) for dy in sorted(range(n_y), key=lambda d: -min(d, n_y - d)) for c in range(2) if dy or c
    ]
    gather_to = [index(cx, cy + dy, lax.rem(core + c, 2)) for dy, c in column]
    rows_to = []
    for m in chunks:
        for j in range(tiles):
            to = m * tiles + j
            slot = lax.rem(to - cy + n_y, n_y)
            rows_to.append((to, slot, index(cx + 1, to, core), index(cx, to, core)))
    barrier = pltpu.get_barrier_semaphore()

    def greet(grid, peer):
        pl.semaphore_signal(barrier, inc=1, device_id=(grid, peer), device_id_type=MESH)

    @pl.when(first)
    def _():
        for dx in range(n_x):
            for dy in range(n_y):
                greet(before, index(cx + dx, cy + dy, core))
        for dy, c in column:
            greet(g, index(cx, cy + dy, (core + c) % 2))
        for dy in range(n_y):
            greet(g, index(cx + 1, cy + dy, core))

    @pl.when(z > 0)
    def _():
        greet(g, partner)

    @pl.when(z < n_z - 2)
    def _():
        for dx in range(n_x):
            for dy in range(n_y):
                greet(after, index(cx + dx, cy + dy, core))

    @pl.when(z == n_z - 2)
    def _():
        greet(after, k)

    for copy in scalars:
        copy.wait()
    count = occ[k]
    whole = kw[core]
    for i in range(1, kw.shape[0] // 2):
        whole = whole + kw[2 * i + core]
    shape = (thick, mine.shape[2])
    scale = jnp.full(shape, kw[k], jnp.int32).astype(jnp.float32) / jnp.full(shape, whole, jnp.int32).astype(jnp.float32)

    def send(src, dst, send_sem, recv_sem, device):
        copy = pltpu.make_async_remote_copy(
            src_ref=src, dst_ref=dst, send_sem=send_sem, recv_sem=recv_sem, device_id=device, device_id_type=MESH
        )
        copy.start()

    def wait_for(ref, sem):
        pltpu.make_async_copy(ref, ref, sem).wait()

    target = jnp.where(first, g, jnp.where(last, after, before))
    source = jnp.where(first, FROM_OWN, jnp.where(last, FROM_BEFORE, FROM_AFTER))
    groups = count // UNROLL
    rest = jnp.minimum(groups * UNROLL, bands - UNROLL)

    def pair_sum(values):
        while len(values) > 1:
            values = [a + b for a, b in zip(values[::2], values[1::2])]
        return values[0]

    for i, m in enumerate(chunks):

        def add(step, sums):
            values = [orb[i][step * UNROLL + j].astype(jnp.float32) for j in range(UNROLL)]
            group = pair_sum([v * v for v in values])
            return sums + jnp.where(step < groups, group, 0.0)

        total = jnp.zeros(shape, jnp.float32)
        for p in range(PARTS):
            loads[i * PARTS + p].wait()
            total = lax.fori_loop(p * half // UNROLL, (p + 1) * half // UNROLL, add, total, unroll=2)
        values = [orb[i][rest + j].astype(jnp.float32) for j in range(UNROLL)]
        total = total + pair_sum([jnp.where(groups * UNROLL + j < count, v * v, 0.0) for j, v in enumerate(values)])
        total = total * scale
        for j in range(tiles):
            part[m * tiles + j] = total[j * tile:(j + 1) * tile]
        if i == 0:
            pl.semaphore_wait(
                barrier, jnp.where(first, 3 * n_y - 1, jnp.where(last, n_x * n_y + 2, n_x * n_y + 1))
            )

        for to, slot, across, along in rows_to[i * tiles:(i + 1) * tiles]:
            send(
                part.at[to], recv.at[source, n_y + slot], rs_send, rs_recv.at[source], (target, across)
            )

            @pl.when((z > 0) | (to != cy))
            def _():
                send(
                    part.at[to], recv.at[source, slot], rs_send, rs_recv.at[source],
                    (target, along),
                )

    whole_set = pl.ds(0, n_x * n_y)
    others = pl.ds(1, n_x * n_y - 1)

    def add_up(which, value):
        return pair_sum([value] + [recv[which, i] for i in range(1, n_x * n_y)])

    def reply(which, what, src, dst, grid, x):
        send(
            mine.at[src], mine.at[dst], reply_send.at[which], reply_recv.at[what], (grid, index(x, cy, core))
        )

    def spread(i, src, ref):
        for peer in gather_to:
            send(mine.at[src], ref.at[core, cy], ag_send.at[i], ag_recv.at[i], (g, peer))
        ref[core, cy] = mine[src]

    @pl.when(z < n_z - 2)
    def _():
        wait_for(recv.at[FROM_AFTER, whole_set], rs_recv.at[FROM_AFTER])
        mine[NEXT] = add_up(FROM_AFTER, recv[FROM_AFTER, 0])
        reply(0, 0, NEXT, OWN, after, cx)

    @pl.when(first)
    def _():
        wait_for(recv.at[FROM_OWN, others], rs_recv.at[FROM_OWN])
        mine[OWN] = add_up(FROM_OWN, part[cy])

    @pl.when(z > 0)
    def _():
        wait_for(mine.at[OWN], reply_recv.at[0])

    pl.semaphore_signal(known, inc=1, device_id=(g, partner), device_id_type=MESH)

    @pl.when(z < n_z - 2)
    def _():
        reply(1, 1, OWN, PREVIOUS, after, cx)

    @pl.when(last)
    def _():
        reply(2, 2, OWN, NEXT, before, cx)

    pl.semaphore_wait(known, 1)
    spread(0, OWN, dens_ref)

    @pl.when(z >= n_z - 2)
    def _():
        wait_for(mine.at[NEXT], reply_recv.at[2])

    @pl.when(z == n_z - 2)
    def _():
        reply(1, 1, OWN, PREVIOUS, after, cx)

    @pl.when(first)
    def _():
        wait_for(recv.at[FROM_BEFORE, whole_set], rs_recv.at[FROM_BEFORE])
        mine[PREVIOUS] = add_up(FROM_BEFORE, recv[FROM_BEFORE, 0])

    @pl.when(z > 0)
    def _():
        wait_for(mine.at[PREVIOUS], reply_recv.at[1])

    mine[SLOPE] = (mine[NEXT] - mine[PREVIOUS]) * 0.5
    spread(1, SLOPE, grad_ref)

    wait_for(recv.at[FROM_OWN, others], ag_recv.at[0])
    prepare(dens_ref, ready)

    @pl.when(first)
    def _():
        reply(3, 0, PREVIOUS, OWN, before, cx + 1)
        reply(2, 2, OWN, NEXT, before, cx + 1)
        wait_for(mine.at[OWN], reply_send.at[3])
        wait_for(recv.at[FROM_OWN, others], rs_send)

    @pl.when(first | last)
    def _():
        wait_for(mine.at[OWN], reply_send.at[2])

    @pl.when(z < n_z - 2)
    def _():
        wait_for(mine.at[OWN], reply_send.at[0])

    @pl.when(z < n_z - 1)
    def _():
        wait_for(mine.at[OWN], reply_send.at[1])

    @pl.when(z > 0)
    def _():
        wait_for(recv.at[FROM_OWN, whole_set], rs_send)

    for i in range(2):
        wait_for(recv.at[FROM_OWN, others], ag_send.at[i])
    wait_for(recv.at[FROM_OWN, others], ag_recv.at[1])
    finish(grad_ref, ready, pot_ref, flux_ref)


def prepare(dens_ref, ready):
    rows, depth = ready.shape[2:]
    pair = [dens_ref[i].reshape(rows, depth) for i in range(2)]
    both = pair[0] + pair[1]
    polar = (pair[0] - pair[1]) / both
    radius = radius_coef * jnp.exp(jnp.log(both) * (-1.0 / 3.0))
    inverse = 1.0 / (radius + 7.8)
    front = -0.44 * inverse
    even = (1.0 - 0.5 * polar * polar) * (1.0 + radius * inverse * (1.0 / 3.0))
    for i, (value, sign) in enumerate(zip(pair, (1.0, -1.0))):
        scaled = 2.0 * value
        cube = jnp.exp(jnp.log(scaled) * (1.0 / 3.0))
        over = 1.0 / (scaled * cube)
        grad_y = (pltpu.roll(value, rows - 1, 0) - pltpu.roll(value, 1, 0)) * 0.5
        grad_z = (pltpu.roll(value, depth - 1, 1) - pltpu.roll(value, 1, 1)) * 0.5
        unit = (4.0 / fermi_term) * over * over
        terms = (
            grad_y,
            grad_z,
            unit,
            unit * (grad_y * grad_y + grad_z * grad_z),
            -exchange_coef * cube,
            front * (even - polar * (sign - polar)),
            (-4.0 * exchange_coef * mu_value / fermi_term) * over,
        )
        for j, term in enumerate(terms):
            ready[i, j] = term


def finish(grad_ref, ready, pot_ref, flux_ref):
    rows, depth = ready.shape[2:]
    for i in range(2):
        grad_x = grad_ref[i].reshape(rows, depth)
        reduced = ready[i, 3] + ready[i, 2] * (grad_x * grad_x)
        ratio = 1.0 / (1.0 + (mu_value / kappa_value) * reduced)
        enhance = 1.0 + kappa_value - kappa_value * ratio
        slope = mu_value * ratio
        pot_ref[pl.ds(i * rows, rows)] = ready[i, 5] + ready[i, 4] * (
            (4.0 / 3.0) * enhance - (8.0 / 3.0) * (reduced * ratio) * slope
        )
        factor = ready[i, 6] * (ratio * ratio)
        for c, term in enumerate((ready[i, 0], grad_x, ready[i, 1])):
            flux_ref[pl.ds(i * 3 * rows + c, rows, stride=3)] = factor * term


def put_kernel(*refs):
    sources, targets, sem = refs[:3], refs[3:6], refs[6]
    copies = [pltpu.make_async_copy(a, b, sem.at[i]) for i, (a, b) in enumerate(zip(sources, targets))]
    for copy in copies[::-1]:
        copy.start()
    for copy in copies:
        copy.wait()


def on_device(n_grid, n_x, n_y, n_z, orbitals, occupied, kweight):
    _, bands, rows, _, depth = orbitals.shape
    local = orbitals.reshape(bands, rows, depth)
    tile = rows // n_y
    out = functools.partial(pltpu.VMEM, dtype=jnp.float32)
    vmem = pl.BlockSpec(memory_space=pltpu.VMEM)
    dma = pltpu.SemaphoreType.DMA
    dens, pot, flux = pl.pallas_call(
        functools.partial(gather_kernel, (n_grid, n_x, n_y, n_z)),
        out_shape=(out((2, n_y, tile, depth)), out((2 * rows, depth)), out((6 * rows, depth))),
        in_specs=[pl.BlockSpec(memory_space=pl.ANY)] * 3,
        out_specs=(vmem,) * 3,
        scratch_shapes=[
            *[pltpu.VMEM((bands, rows // CHUNKS, depth), jnp.bfloat16) for _ in range(CHUNKS)],
            pltpu.SMEM(occupied.shape, jnp.int32),
            pltpu.SMEM(kweight.shape, jnp.int32),
            pltpu.VMEM((n_y, tile, depth), jnp.float32),
            pltpu.VMEM((3, 2 * n_y, tile, depth), jnp.float32),
            pltpu.VMEM((4, tile, depth), jnp.float32),
            pltpu.VMEM((2, n_y, tile, depth), jnp.float32),
            pltpu.VMEM((2, 7, rows, depth), jnp.float32),
            dma((CHUNKS * PARTS,)),
            dma((2,)),
            dma(()),
            dma((3,)),
            dma((4,)),
            dma((3,)),
            dma((2,)),
            dma((2,)),
            pltpu.SemaphoreType.REGULAR,
        ],
        compiler_params=pltpu.CompilerParams(
            collective_id=0, has_side_effects=True, vmem_limit_bytes=VMEM_LIMIT
        ),
        name="density",
    )(local, occupied, kweight)
    parts = (dens.reshape(2 * rows, depth), pot, flux)
    outs = pl.pallas_call(
        put_kernel,
        out_shape=[jax.ShapeDtypeStruct(part.shape, part.dtype) for part in parts],
        in_specs=[vmem] * 3,
        out_specs=[pl.BlockSpec(memory_space=pl.ANY)] * 3,
        scratch_shapes=[dma((3,))],
        compiler_params=pltpu.CompilerParams(vmem_limit_bytes=8 << 20),
        name="put",
    )(*parts)
    return (
        outs[0].reshape(2, rows, 1, depth),
        outs[1].reshape(2, rows, 1, depth),
        outs[2].reshape(2, rows, 3, 1, depth),
    )


def solution(mesh):
    n_grid, n_ks = mesh.shape["grid"], mesh.shape["ks"]
    placed = (P("ks", None, None, "grid", None), P(), P())
    return jax.shard_map(
        functools.partial(on_device, n_grid, 2, n_ks // 4, n_grid // 2),
        mesh=mesh,
        in_specs=placed,
        out_specs=(
            P(None, None, "grid", None),
            P(None, None, "grid", None),
            P(None, None, None, "grid", None),
        ),
        check_vma=False,
    )
```

```python
import functools
import math

import jax
import jax.numpy as jnp
from jax import lax
from jax.experimental import pallas as pl
from jax.experimental.pallas import tpu as pltpu
from jax.sharding import PartitionSpec as P

MESH = pl.DeviceIdType.MESH
CHUNKS = 4
UNROLL = 8
PARTS = 2
VMEM_LIMIT = 62 << 20

exchange_coef = 0.75 * (3.0 / math.pi) ** (1.0 / 3.0)
kappa_value = 0.804
mu_value = 0.2195
fermi_term = 4.0 * (3.0 * math.pi * math.pi) ** (2.0 / 3.0)
radius_coef = (3.0 / (4.0 * math.pi)) ** (1.0 / 3.0)


def gather_kernel(
    sizes, orb_hbm, occ_hbm, kw_hbm, dens_ref, pot_ref, flux_ref,
    *scratch,
):
    orb = scratch[:CHUNKS]
    (
        occ, kw, part, recv, mine, grad_ref, ready,
        load_sem, scalar_sem, rs_send, rs_recv, reply_send, reply_recv, ag_send, ag_recv, known,
    ) = scratch[CHUNKS:]
    n_grid, n_x, n_y, n_z = sizes
    bands, rows = orb_hbm.shape[:2]
    g = lax.axis_index("grid")
    k = lax.axis_index("ks")
    core = k % 2
    chip = k // 2
    cx, cy = chip // n_y, chip % n_y
    z = g % n_z
    first, last = z == 0, z == n_z - 1
    after, before = (g + 1) % n_grid, (g + n_grid - 1) % n_grid
    tile = rows // n_y
    thick = rows // CHUNKS
    tiles = n_y // CHUNKS
    FROM_AFTER, FROM_OWN, FROM_BEFORE = 0, 1, 2
    OWN, NEXT, PREVIOUS, SLOPE = 0, 1, 2, 3

    turns = sorted(range(CHUNKS), key=lambda m: -min(m, CHUNKS - m))
    chunks = [(cy // tiles + m) % CHUNKS for m in turns]
    half = bands // PARTS
    loads = [
        pltpu.make_async_copy(
            orb_hbm.at[pl.ds(p * half, half), pl.ds(pl.multiple_of(m * thick, thick), thick)],
            orb[i].at[pl.ds(p * half, half)],
            load_sem.at[i * PARTS + p],
        )
        for i, m in enumerate(chunks)
        for p in range(PARTS)
    ]
    scalars = [
        pltpu.make_async_copy(occ_hbm, occ, scalar_sem.at[0]),
        pltpu.make_async_copy(kw_hbm, kw, scalar_sem.at[1]),
    ]
    for copy in loads[:1] + scalars + loads[1:]:
        copy.start()

    def index(x, y, c):
        return (lax.rem(x, n_x) * n_y + lax.rem(y, n_y)) * 2 + c

    partner = index(cx, cy, 1 - core)
    column = [
        (dy, c) for c in (1, 0) for dy in sorted(range(n_y), key=lambda d: -min(d, n_y - d)) if dy or c
    ]
    gather_to = [index(cx, cy + dy, lax.rem(core + c, 2)) for dy, c in column]
    rows_to = []
    for m in chunks:
        for j in range(tiles):
            to = m * tiles + j
            slot = lax.rem(to - cy + n_y, n_y)
            rows_to.append((to, slot, index(cx + 1, to, core), index(cx, to, core)))
    barrier = pltpu.get_barrier_semaphore()

    def greet(grid, peer):
        pl.semaphore_signal(barrier, inc=1, device_id=(grid, peer), device_id_type=MESH)

    @pl.when(first)
    def _():
        for dx in range(n_x):
            for dy in range(n_y):
                greet(before, index(cx + dx, cy + dy, core))
        for dy, c in column:
            greet(g, index(cx, cy + dy, (core + c) % 2))
        for dy in range(n_y):
            greet(g, index(cx + 1, cy + dy, core))

    @pl.when(z > 0)
    def _():
        greet(g, partner)

    @pl.when(z < n_z - 2)
    def _():
        for dx in range(n_x):
            for dy in range(n_y):
                greet(after, index(cx + dx, cy + dy, core))

    @pl.when(z == n_z - 2)
    def _():
        greet(after, k)

    for copy in scalars:
        copy.wait()
    count = occ[k]
    whole = kw[core]
    for i in range(1, kw.shape[0] // 2):
        whole = whole + kw[2 * i + core]
    shape = (thick, mine.shape[2])
    scale = jnp.full(shape, kw[k], jnp.int32).astype(jnp.float32) / jnp.full(shape, whole, jnp.int32).astype(jnp.float32)

    def send(src, dst, send_sem, recv_sem, device):
        copy = pltpu.make_async_remote_copy(
            src_ref=src, dst_ref=dst, send_sem=send_sem, recv_sem=recv_sem, device_id=device, device_id_type=MESH
        )
        copy.start()

    def wait_for(ref, sem):
        pltpu.make_async_copy(ref, ref, sem).wait()

    target = jnp.where(first, g, jnp.where(last, after, before))
    source = jnp.where(first, FROM_OWN, jnp.where(last, FROM_BEFORE, FROM_AFTER))
    groups = count // UNROLL
    rest = jnp.minimum(groups * UNROLL, bands - UNROLL)

    def pair_sum(values):
        while len(values) > 1:
            values = [a + b for a, b in zip(values[::2], values[1::2])]
        return values[0]

    for i, m in enumerate(chunks):

        def add(step, sums):
            values = [orb[i][step * UNROLL + j].astype(jnp.float32) for j in range(UNROLL)]
            group = pair_sum([v * v for v in values])
            return sums + jnp.where(step < groups, group, 0.0)

        total = jnp.zeros(shape, jnp.float32)
        for p in range(PARTS):
            loads[i * PARTS + p].wait()
            total = lax.fori_loop(p * half // UNROLL, (p + 1) * half // UNROLL, add, total, unroll=2)
        values = [orb[i][rest + j].astype(jnp.float32) for j in range(UNROLL)]
        total = total + pair_sum([jnp.where(groups * UNROLL + j < count, v * v, 0.0) for j, v in enumerate(values)])
        total = total * scale
        for j in range(tiles):
            part[m * tiles + j] = total[j * tile:(j + 1) * tile]
        if i == 0:
            pl.semaphore_wait(
                barrier, jnp.where(first, 3 * n_y - 1, jnp.where(last, n_x * n_y + 2, n_x * n_y + 1))
            )

        for to, slot, across, along in rows_to[i * tiles:(i + 1) * tiles]:
            send(
                part.at[to], recv.at[source, n_y + slot], rs_send, rs_recv.at[source], (target, across)
            )

            @pl.when((z > 0) | (to != cy))
            def _():
                send(
                    part.at[to], recv.at[source, slot], rs_send, rs_recv.at[source],
                    (target, along),
                )

    whole_set = pl.ds(0, n_x * n_y)
    others = pl.ds(1, n_x * n_y - 1)

    def add_up(which, value):
        return pair_sum([value] + [recv[which, i] for i in range(1, n_x * n_y)])

    def reply(which, what, src, dst, grid, x):
        send(
            mine.at[src], mine.at[dst], reply_send.at[which], reply_recv.at[what], (grid, index(x, cy, core))
        )

    def spread(i, src, ref):
        for peer in gather_to:
            send(mine.at[src], ref.at[core, cy], ag_send.at[i], ag_recv.at[i], (g, peer))
        ref[core, cy] = mine[src]

    @pl.when(z < n_z - 2)
    def _():
        wait_for(recv.at[FROM_AFTER, whole_set], rs_recv.at[FROM_AFTER])
        mine[NEXT] = add_up(FROM_AFTER, recv[FROM_AFTER, 0])
        reply(0, 0, NEXT, OWN, after, cx)

    @pl.when(first)
    def _():
        wait_for(recv.at[FROM_OWN, others], rs_recv.at[FROM_OWN])
        mine[OWN] = add_up(FROM_OWN, part[cy])

    @pl.when(z > 0)
    def _():
        wait_for(mine.at[OWN], reply_recv.at[0])

    pl.semaphore_signal(known, inc=1, device_id=(g, partner), device_id_type=MESH)

    @pl.when(z < n_z - 2)
    def _():
        reply(1, 1, OWN, PREVIOUS, after, cx)

    @pl.when(last)
    def _():
        reply(2, 2, OWN, NEXT, before, cx)

    pl.semaphore_wait(known, 1)
    spread(0, OWN, dens_ref)

    @pl.when(z >= n_z - 2)
    def _():
        wait_for(mine.at[NEXT], reply_recv.at[2])

    @pl.when(z == n_z - 2)
    def _():
        reply(1, 1, OWN, PREVIOUS, after, cx)

    @pl.when(first)
    def _():
        wait_for(recv.at[FROM_BEFORE, whole_set], rs_recv.at[FROM_BEFORE])
        mine[PREVIOUS] = add_up(FROM_BEFORE, recv[FROM_BEFORE, 0])

    @pl.when(z > 0)
    def _():
        wait_for(mine.at[PREVIOUS], reply_recv.at[1])

    mine[SLOPE] = (mine[NEXT] - mine[PREVIOUS]) * 0.5
    spread(1, SLOPE, grad_ref)

    wait_for(recv.at[FROM_OWN, others], ag_recv.at[0])
    prepare(dens_ref, ready)

    @pl.when(first)
    def _():
        reply(3, 0, PREVIOUS, OWN, before, cx + 1)
        reply(2, 2, OWN, NEXT, before, cx + 1)
        wait_for(mine.at[OWN], reply_send.at[3])
        wait_for(recv.at[FROM_OWN, others], rs_send)

    @pl.when(first | last)
    def _():
        wait_for(mine.at[OWN], reply_send.at[2])

    @pl.when(z < n_z - 2)
    def _():
        wait_for(mine.at[OWN], reply_send.at[0])

    @pl.when(z < n_z - 1)
    def _():
        wait_for(mine.at[OWN], reply_send.at[1])

    @pl.when(z > 0)
    def _():
        wait_for(recv.at[FROM_OWN, whole_set], rs_send)

    for i in range(2):
        wait_for(recv.at[FROM_OWN, others], ag_send.at[i])
    wait_for(recv.at[FROM_OWN, others], ag_recv.at[1])
    finish(grad_ref, ready, pot_ref, flux_ref)


def prepare(dens_ref, ready):
    rows, depth = ready.shape[2:]
    pair = [dens_ref[i].reshape(rows, depth) for i in range(2)]
    both = pair[0] + pair[1]
    polar = (pair[0] - pair[1]) / both
    radius = radius_coef * jnp.exp(jnp.log(both) * (-1.0 / 3.0))
    inverse = 1.0 / (radius + 7.8)
    front = -0.44 * inverse
    even = (1.0 - 0.5 * polar * polar) * (1.0 + radius * inverse * (1.0 / 3.0))
    for i, (value, sign) in enumerate(zip(pair, (1.0, -1.0))):
        scaled = 2.0 * value
        cube = jnp.exp(jnp.log(scaled) * (1.0 / 3.0))
        over = 1.0 / (scaled * cube)
        grad_y = (pltpu.roll(value, rows - 1, 0) - pltpu.roll(value, 1, 0)) * 0.5
        grad_z = (pltpu.roll(value, depth - 1, 1) - pltpu.roll(value, 1, 1)) * 0.5
        unit = (4.0 / fermi_term) * over * over
        terms = (
            grad_y,
            grad_z,
            unit,
            unit * (grad_y * grad_y + grad_z * grad_z),
            -exchange_coef * cube,
            front * (even - polar * (sign - polar)),
            (-4.0 * exchange_coef * mu_value / fermi_term) * over,
        )
        for j, term in enumerate(terms):
            ready[i, j] = term


def finish(grad_ref, ready, pot_ref, flux_ref):
    rows, depth = ready.shape[2:]
    for i in range(2):
        grad_x = grad_ref[i].reshape(rows, depth)
        reduced = ready[i, 3] + ready[i, 2] * (grad_x * grad_x)
        ratio = 1.0 / (1.0 + (mu_value / kappa_value) * reduced)
        enhance = 1.0 + kappa_value - kappa_value * ratio
        slope = mu_value * ratio
        pot_ref[pl.ds(i * rows, rows)] = ready[i, 5] + ready[i, 4] * (
            (4.0 / 3.0) * enhance - (8.0 / 3.0) * (reduced * ratio) * slope
        )
        factor = ready[i, 6] * (ratio * ratio)
        for c, term in enumerate((ready[i, 0], grad_x, ready[i, 1])):
            flux_ref[pl.ds(i * 3 * rows + c, rows, stride=3)] = factor * term


def put_kernel(*refs):
    sources, targets, sem = refs[:3], refs[3:6], refs[6]
    copies = [pltpu.make_async_copy(a, b, sem.at[i]) for i, (a, b) in enumerate(zip(sources, targets))]
    for copy in copies[::-1]:
        copy.start()
    for copy in copies:
        copy.wait()


def on_device(n_grid, n_x, n_y, n_z, orbitals, occupied, kweight):
    _, bands, rows, _, depth = orbitals.shape
    local = orbitals.reshape(bands, rows, depth)
    tile = rows // n_y
    out = functools.partial(pltpu.VMEM, dtype=jnp.float32)
    vmem = pl.BlockSpec(memory_space=pltpu.VMEM)
    dma = pltpu.SemaphoreType.DMA
    dens, pot, flux = pl.pallas_call(
        functools.partial(gather_kernel, (n_grid, n_x, n_y, n_z)),
        out_shape=(out((2, n_y, tile, depth)), out((2 * rows, depth)), out((6 * rows, depth))),
        in_specs=[pl.BlockSpec(memory_space=pl.ANY)] * 3,
        out_specs=(vmem,) * 3,
        scratch_shapes=[
            *[pltpu.VMEM((bands, rows // CHUNKS, depth), jnp.bfloat16) for _ in range(CHUNKS)],
            pltpu.SMEM(occupied.shape, jnp.int32),
            pltpu.SMEM(kweight.shape, jnp.int32),
            pltpu.VMEM((n_y, tile, depth), jnp.float32),
            pltpu.VMEM((3, 2 * n_y, tile, depth), jnp.float32),
            pltpu.VMEM((4, tile, depth), jnp.float32),
            pltpu.VMEM((2, n_y, tile, depth), jnp.float32),
            pltpu.VMEM((2, 7, rows, depth), jnp.float32),
            dma((CHUNKS * PARTS,)),
            dma((2,)),
            dma(()),
            dma((3,)),
            dma((4,)),
            dma((3,)),
            dma((2,)),
            dma((2,)),
            pltpu.SemaphoreType.REGULAR,
        ],
        compiler_params=pltpu.CompilerParams(
            collective_id=0, has_side_effects=True, vmem_limit_bytes=VMEM_LIMIT
        ),
        name="density",
    )(local, occupied, kweight)
    parts = (dens.reshape(2 * rows, depth), pot, flux)
    outs = pl.pallas_call(
        put_kernel,
        out_shape=[jax.ShapeDtypeStruct(part.shape, part.dtype) for part in parts],
        in_specs=[vmem] * 3,
        out_specs=[pl.BlockSpec(memory_space=pl.ANY)] * 3,
        scratch_shapes=[dma((3,))],
        compiler_params=pltpu.CompilerParams(vmem_limit_bytes=8 << 20),
        name="put",
    )(*parts)
    return (
        outs[0].reshape(2, rows, 1, depth),
        outs[1].reshape(2, rows, 1, depth),
        outs[2].reshape(2, rows, 3, 1, depth),
    )


def solution(mesh):
    n_grid, n_ks = mesh.shape["grid"], mesh.shape["ks"]
    placed = (P("ks", None, None, "grid", None), P(), P())
    return jax.shard_map(
        functools.partial(on_device, n_grid, 2, n_ks // 4, n_grid // 2),
        mesh=mesh,
        in_specs=placed,
        out_specs=(
            P(None, None, "grid", None),
            P(None, None, "grid", None),
            P(None, None, None, "grid", None),
        ),
        check_vma=False,
    )
```
